32 devices in a mesh: fsdp: 4 (over x, core), expert: 8 (over z, y).
Axes of the slice: x: 2, y: 2, z: 4, core: 2. Of those that a mesh axis runs over, the one named last changes fastest.
Arguments:
- tokens: bfloat16 [32, 197, 768], P(('fsdp', 'expert')), may hold values from -6 to 6
- expert_ids: int32 [32, 197, 2], P(('fsdp', 'expert')), may hold values from 0 to 7, all different within a row
- ln1_gain: bfloat16 [768], P(('fsdp', 'expert')), may hold values from 0.5 to 1.5
- w_qkv: bfloat16 [768, 2304], P(('fsdp', 'expert')), may hold values from -0.21875 to 0.21875
- w_out: bfloat16 [768, 768], P(('fsdp', 'expert')), may hold values from -1.75 to 1.75
- ln2_gain: bfloat16 [768], P(('fsdp', 'expert')), may hold values from 0.5 to 1.5
- w_router: bfloat16 [768, 8], P(('fsdp', 'expert')), may hold values from -0.21875 to 0.21875
- w_in: bfloat16 [8, 768, 3072], P('expert', 'fsdp'), may hold values from -0.21875 to 0.21875
- w_back: bfloat16 [8, 3072, 768], P('expert', 'fsdp'), may hold values from -2.5 to 2.5
- cotangent: bfloat16 [32, 197, 768], P(('fsdp', 'expert')), may hold values from -6 to 6
Outputs:
- block_out: bfloat16 [32, 197, 768], P(('fsdp', 'expert'))
- grad_tokens: float32 [32, 197, 768], P(('fsdp', 'expert'))
- grad_ln1: float32 [768], P(('fsdp', 'expert'))
- grad_qkv: float32 [768, 2304], P(('fsdp', 'expert'))
- grad_out: float32 [768, 768], P(('fsdp', 'expert'))
- grad_ln2: float32 [768], P(('fsdp', 'expert'))
- grad_router: float32 [768, 8], P(('fsdp', 'expert'))
- grad_in: float32 [8, 768, 3072], P('expert', 'fsdp')
- grad_back: float32 [8, 3072, 768], P('expert', 'fsdp')
The draws below stay inside these ranges and needn't reach their ends.
Inputs may be any that keep to these rules, and one draw needn't show every extreme that they name: `expert_ids`: each token's two entries name different experts.
All inputs are finite; a program needn't handle non-finite values.
Results may differ from the reference program's by a relative error of at most 0.015.
Values may be sent and summed in bfloat16 or wider, within the bound.
No kernel may reach another device: no remote copies, remote signals or barrier semaphores. Data moves between devices by JAX's collectives and lax.ppermute only.
A program may use at most 128 MiB of HBM per device.

```python
import math
import jax
import jax.numpy as jnp
from jax import lax

D = 768
HEADS = 12
HD = 64
FF = 3072
S = 197
IMG_DEV = 1
E = 8
CAP = 8
IMAGES = 32


def block_levels(stream_key, shape, cuts, smallest, high):
    def one(position, blocks):
        draws = jax.random.uniform(jax.random.fold_in(jax.random.fold_in(stream_key, 6), position), (blocks,), jnp.float32, smallest / len(cuts), high / len(cuts))
        return jnp.repeat(jnp.exp(draws), shape[position] // blocks).reshape((-1,) + (1,) * (len(shape) - position - 1))

    loudness = one(*cuts[0])
    for cut in cuts[1:]:
        loudness = loudness * one(*cut)
    return loudness


def choose_distinct(key, rows, amount, top, lift):
    ranking = jax.random.permutation(jax.random.fold_in(key, 1), amount)
    pull = ranking
    for power in range(3):
        pull = pull * pull // amount
    pull = pull * lift // amount
    chance = jax.random.randint(jax.random.fold_in(key, 2), (rows, amount), 0, 4096) + pull
    fixed_rows = jax.random.permutation(jax.random.fold_in(key, 3), rows)[jnp.arange(amount) % rows]
    chance = jnp.where(jnp.arange(rows)[:, None] == fixed_rows[None, :], 1 << 14, chance)
    score = chance * amount + jnp.arange(amount)
    return lax.top_k(score.astype(jnp.int32), top)[1].astype(jnp.int32)


def gaussian(rng, extent, spread, reach, shards=(), held_as=jnp.bfloat16):
    factor_of = block_levels(rng, extent, shards, -0.22, 0.18) if shards else 1.0
    values = jax.random.normal(rng, extent, jnp.float32) * spread * factor_of
    return jnp.minimum(jnp.maximum(values, -reach), reach).astype(held_as)


def setup_inputs(seed: int = 0) -> dict:
    splits = jax.random.split(jax.random.key(seed), 11)
    tokens = gaussian(splits[0], (IMAGES, S, D), 1.0, 6.0, ((0, 32),))
    expert_ids = choose_distinct(splits[1], IMAGES * S, E, 2, 2048).reshape((IMAGES, S, 2))
    ln1_gain = jnp.clip(1.0 + 0.1 * jax.random.normal(splits[2], (D,), jnp.float32), 0.5, 1.5).astype(jnp.bfloat16)
    w_qkv = gaussian(splits[3], (D, 3 * D), D ** -0.5, 0.21875, ((0, 32),))
    w_out = gaussian(splits[4], (D, D), (max(4, D // 64)) ** -0.5, 1.75, ((0, 32),))
    ln2_gain = jnp.clip(1.0 + 0.1 * jax.random.normal(splits[5], (D,), jnp.float32), 0.5, 1.5).astype(jnp.bfloat16)
    w_router = gaussian(splits[6], (D, E), D ** -0.5, 0.21875, ((0, 32),))
    w_in = gaussian(splits[7], (E, D, FF), D ** -0.5, 0.21875, ((0, 8), (1, 4)))
    w_back = gaussian(splits[8], (E, FF, D), (max(4, FF // 512)) ** -0.5, 2.5, ((0, 8), (1, 4)))
    cotangent = gaussian(splits[9], (IMAGES, S, D), 1.0, 6.0, ((0, 32),))
    return dict(tokens=tokens, expert_ids=expert_ids, ln1_gain=ln1_gain, w_qkv=w_qkv, w_out=w_out, ln2_gain=ln2_gain, w_router=w_router, w_in=w_in, w_back=w_back, cotangent=cotangent)


EPS = 1e-06
ROOT_HALF = 0.7071067811865476
INV_ROOT_TAU = 0.3989422804014327

def rounded(values):
    return lax.optimization_barrier(values.astype(jnp.bfloat16)).astype(jnp.float32)

def normalize(values):
    average = lax.optimization_barrier(jnp.mean(values, axis=-1, keepdims=True))
    centered = values - average
    variance = lax.optimization_barrier(jnp.mean(centered * centered, axis=-1, keepdims=True))
    inv_std = lax.rsqrt(variance + EPS)
    return (centered * inv_std, inv_std)

def norm_back(d_normed, normed, inv_std, gain):
    d_scaled = d_normed * gain
    d_gain = lax.optimization_barrier(jnp.sum(d_normed * normed, axis=0))
    d_values = (d_scaled - lax.optimization_barrier(jnp.mean(d_scaled, axis=-1, keepdims=True)) - normed * lax.optimization_barrier(jnp.mean(d_scaled * normed, axis=-1, keepdims=True))) * inv_std
    return (d_values, d_gain)

def normal_cdf(values):
    return 0.5 * (1.0 + lax.erf(values * ROOT_HALF))

def gelu_exact(values):
    return values * normal_cdf(values)

def gelu_slope(values):
    return normal_cdf(values) + values * jnp.exp(-0.5 * values * values) * INV_ROOT_TAU

def slot_layout(chosen, experts, capacity):
    row_count = chosen.shape[0]
    flat_ids = jnp.concatenate([chosen[:, 0], chosen[:, 1]]).astype(jnp.int32)
    one_hot = (flat_ids[:, None] == jnp.arange(experts, dtype=jnp.int32)[None, :]).astype(jnp.int32)
    earlier = jnp.cumsum(one_hot, axis=0) - one_hot
    slot_pos = lax.optimization_barrier(jnp.sum(earlier * one_hot, axis=1)).astype(jnp.int32)
    is_kept = slot_pos < capacity
    target = jnp.where(is_kept, flat_ids * capacity + slot_pos, experts * capacity).astype(jnp.int32)
    token_idx = jnp.concatenate([jnp.arange(row_count, dtype=jnp.int32)] * 2)
    source = jnp.full((experts * capacity,), row_count, jnp.int32).at[target].set(token_idx, mode='drop')
    return (target.reshape(2, row_count), is_kept.reshape(2, row_count), source)

def reference(tokens, expert_ids, ln1_gain, w_qkv, w_out, ln2_gain, w_router, w_in, w_back, cotangent):
    row_count = IMG_DEV * S
    groups = IMAGES // IMG_DEV
    score_scale = 1.0 / math.sqrt(HD)
    gain_one = ln1_gain.astype(jnp.float32)
    gain_two = ln2_gain.astype(jnp.float32)
    in_wide = w_in.astype(jnp.float32)
    back_wide = w_back.astype(jnp.float32)

    def one_block(carry, inputs):
        block_x, block_ids, block_cot = inputs
        flat_x = block_x.reshape(row_count, D).astype(jnp.float32)
        normed_one, inv_one = normalize(flat_x)
        input_one = (normed_one * gain_one).astype(jnp.bfloat16)
        projected = rounded(jnp.dot(input_one, w_qkv, preferred_element_type=jnp.float32))
        queries = projected[:, :D].reshape(IMG_DEV, S, HEADS, HD)
        keys_all = projected[:, D:2 * D].reshape(IMG_DEV, S, HEADS, HD)
        values_all = projected[:, 2 * D:].reshape(IMG_DEV, S, HEADS, HD)
        scores = jnp.einsum('ishd,ithd->ihst', queries, keys_all) * score_scale
        log_total = jnp.log(lax.optimization_barrier(jnp.sum(jnp.exp(scores), axis=-1, keepdims=True)))
        weights = jnp.exp(scores - log_total)
        weights_low = rounded(weights)
        mixed_low = jnp.einsum('ihst,ithd->ishd', weights_low, values_all).reshape(row_count, D).astype(jnp.bfloat16)
        attended = jnp.dot(mixed_low, w_out, preferred_element_type=jnp.float32)
        middle = flat_x + attended
        normed_two, inv_two = normalize(middle)
        input_two = (normed_two * gain_two).astype(jnp.bfloat16)
        logits = jnp.dot(input_two, w_router, preferred_element_type=jnp.float32)
        exp_logits = jnp.exp(logits)
        probs = exp_logits / lax.optimization_barrier(jnp.sum(exp_logits, axis=-1, keepdims=True))
        choice_hot = (block_ids[:, :, None] == jnp.arange(E, dtype=jnp.int32)[None, None, :]).astype(jnp.float32)
        gates = lax.optimization_barrier(jnp.sum(probs[:, None, :] * choice_hot, axis=-1)).T
        target, is_kept, source = slot_layout(block_ids, E, CAP)
        kept_mask = is_kept.astype(jnp.float32)
        slot_gate = jnp.zeros((E * CAP,), jnp.float32).at[target.reshape(-1)].set(gates.reshape(-1), mode='drop')
        padded_in = jnp.concatenate([input_two, jnp.zeros((1, D), jnp.bfloat16)])
        expert_rows = padded_in[source].reshape(E, CAP, D).astype(jnp.float32)
        hidden_pre = jnp.einsum('ecd,edf->ecf', expert_rows, in_wide)
        activated = rounded(gelu_exact(hidden_pre))
        expert_out = rounded(jnp.einsum('ecf,efd->ecd', activated, back_wide)).reshape(E * CAP, D)
        padded_out = jnp.concatenate([expert_out, jnp.zeros((1, D), jnp.float32)])
        picked = padded_out[target]
        combined = lax.optimization_barrier(jnp.sum((kept_mask * gates)[:, :, None] * picked, axis=0))
        out_block = (middle + combined).astype(jnp.bfloat16)
        d_final = block_cot.reshape(row_count, D).astype(jnp.float32)
        d_gates = kept_mask * lax.optimization_barrier(jnp.sum(d_final[None] * picked, axis=-1))
        padded_d = jnp.concatenate([d_final, jnp.zeros((1, D), jnp.float32)])
        d_expert_out = rounded(padded_d[source] * slot_gate[:, None]).reshape(E, CAP, D)
        d_activated = jnp.einsum('ecd,efd->ecf', d_expert_out, back_wide)
        d_hidden = rounded(d_activated * gelu_slope(hidden_pre))
        d_rows = rounded(jnp.einsum('ecf,edf->ecd', d_hidden, in_wide)).reshape(E * CAP, D)
        grad_back_part = jnp.einsum('ecf,ecd->efd', activated, d_expert_out)
        grad_in_part = jnp.einsum('ecd,ecf->edf', expert_rows, d_hidden)
        padded_rows = jnp.concatenate([d_rows, jnp.zeros((1, D), jnp.float32)])
        d_input_two = lax.optimization_barrier(jnp.sum(padded_rows[target], axis=0))
        d_probs = lax.optimization_barrier(jnp.sum(d_gates.T[:, :, None] * choice_hot, axis=1))
        d_logits = (probs * (d_probs - lax.optimization_barrier(jnp.sum(probs * d_probs, axis=-1, keepdims=True)))).astype(jnp.bfloat16)
        d_input_two = d_input_two + jnp.dot(d_logits, w_router.T, preferred_element_type=jnp.float32)
        grad_router_part = jnp.dot(input_two.T, d_logits, preferred_element_type=jnp.float32)
        d_norm_two, grad_two_part = norm_back(d_input_two, normed_two, inv_two, gain_two)
        d_middle = d_final + d_norm_two
        d_middle_low = d_middle.astype(jnp.bfloat16)
        grad_out_part = jnp.dot(mixed_low.T, d_middle_low, preferred_element_type=jnp.float32)
        d_mixed = rounded(jnp.dot(d_middle_low, w_out.T, preferred_element_type=jnp.float32)).reshape(IMG_DEV, S, HEADS, HD)
        mixed_wide = mixed_low.astype(jnp.float32).reshape(IMG_DEV, S, HEADS, HD)
        delta = jnp.transpose(lax.optimization_barrier(jnp.sum(d_mixed * mixed_wide, axis=-1)), (0, 2, 1))[..., None]
        d_values = jnp.einsum('ihst,ishd->ithd', weights_low, d_mixed)
        d_weights = jnp.einsum('ishd,ithd->ihst', d_mixed, values_all)
        d_scores = rounded(weights * (d_weights - delta))
        d_queries = jnp.einsum('ihst,ithd->ishd', d_scores, keys_all) * score_scale
        d_keys = jnp.einsum('ihst,ishd->ithd', d_scores, queries) * score_scale
        d_projected = jnp.concatenate([d_queries.reshape(row_count, D), d_keys.reshape(row_count, D), d_values.reshape(row_count, D)], axis=1).astype(jnp.bfloat16)
        grad_qkv_part = jnp.dot(input_one.T, d_projected, preferred_element_type=jnp.float32)
        d_input_one = jnp.dot(d_projected, w_qkv.T, preferred_element_type=jnp.float32)
        d_norm_one, grad_one_part = norm_back(d_input_one, normed_one, inv_one, gain_one)
        d_tokens = d_middle + d_norm_one
        parts = (grad_one_part, grad_qkv_part, grad_out_part, grad_two_part, grad_router_part, grad_in_part, grad_back_part)
        new_carry = tuple((total + part for total, part in zip(carry, parts)))
        return (new_carry, (out_block, d_tokens))
    start_carry = (jnp.zeros((D,), jnp.float32), jnp.zeros((D, 3 * D), jnp.float32), jnp.zeros((D, D), jnp.float32), jnp.zeros((D,), jnp.float32), jnp.zeros((D, E), jnp.float32), jnp.zeros((E, D, FF), jnp.float32), jnp.zeros((E, FF, D), jnp.float32))
    inputs = (tokens.reshape(groups, IMG_DEV, S, D), expert_ids.reshape(groups, row_count, 2), cotangent.reshape(groups, IMG_DEV, S, D))
    totals, stacked = lax.scan(one_block, start_carry, inputs)
    outputs, d_inputs = stacked
    return (outputs.reshape(IMAGES, S, D), d_inputs.reshape(IMAGES, S, D), totals[0], totals[1], totals[2], totals[3], totals[4], totals[5], totals[6])
```

```python
import math

import jax
import jax.numpy as jnp
from jax import lax
from jax.sharding import PartitionSpec as P

HEADS = 12
HD = 64
CAP = 8
LANES = 128

EPS = 1e-06
ROOT_HALF = 0.7071067811865476
INV_ROOT_TAU = 0.3989422804014327

AXES = ("fsdp", "expert")


def normalize(values):
    average = jnp.mean(values, axis=-1, keepdims=True)
    centered = values - average
    variance = jnp.mean(centered * centered, axis=-1, keepdims=True)
    inv_std = lax.rsqrt(variance + EPS)
    return (centered * inv_std, inv_std)


def norm_back(d_normed, normed, inv_std, gain):
    d_scaled = d_normed * gain
    d_gain = jnp.sum(d_normed * normed, axis=0)
    d_values = (
        d_scaled
        - jnp.mean(d_scaled, axis=-1, keepdims=True)
        - normed * jnp.mean(d_scaled * normed, axis=-1, keepdims=True)
    ) * inv_std
    return (d_values, d_gain)


def normal_cdf(values):
    return 0.5 * (1.0 + lax.erf(values * ROOT_HALF))


def dot(left, right, left_dim, right_dim, out=jnp.float32):
    return lax.dot_general(
        left,
        right,
        (((left_dim,), (right_dim,)), ((), ())),
        preferred_element_type=jnp.float32,
    ).astype(out)


def pad_lanes(values):
    extra = -values.shape[-1] % LANES
    return jnp.pad(values, ((0, 0), (0, extra)))


def half_cut(columns):
    return LANES * ((columns // LANES + 1) // 2)


class Cube:
    def __init__(self, fsdp, experts):
        self.count = fsdp * experts
        self.low = experts.bit_length() - 1
        self.bits = self.count.bit_length() - 1
        core = self.low
        across = list(range(self.low + 1, self.bits))
        upper = list(range(self.low - 1, 0, -1))
        lowest = [0] if self.low else []
        self.shared = upper
        self.first = lowest + across
        self.second = across + lowest
        self.core = core if fsdp > 1 else None

    def swap(self, values, bit):
        pairs = [(i, i ^ (1 << bit)) for i in range(self.count)]
        return lax.ppermute(values, AXES, pairs)

    def mine(self, bit):
        index = lax.axis_index(AXES)
        return (index >> bit) & 1

    def grow(self, values, have, bit):
        other = self.swap(values, bit)
        flag = self.mine(bit) == 0
        place = sum(1 for b in have if b > bit)
        low = jnp.where(flag, values, other)
        high = jnp.where(flag, other, values)
        return jnp.stack([low, high], axis=place), have + [bit]

    def gather(self, block):
        rows, columns = block.shape
        have = []
        for bit in self.shared:
            block, have = self.grow(block, have, bit)
        cut = half_cut(columns)
        parts = []
        for piece, order in ((block[..., :cut], self.first), (block[..., cut:], self.second)):
            held = list(have)
            for bit in order:
                piece, held = self.grow(piece, held, bit)
            parts.append(piece)
        whole = jnp.concatenate(parts, axis=-1)
        if self.core is not None:
            whole, held = self.grow(whole, held, self.core)
        return whole.reshape(self.count * rows, columns)

    def shrink(self, values, have, bit):
        place = sum(1 for b in have if b > bit)
        mine = self.mine(bit)
        keep = lax.dynamic_index_in_dim(values, mine, place, keepdims=False)
        give = lax.dynamic_index_in_dim(values, 1 - mine, place, keepdims=False)
        got = self.swap(give.astype(jnp.bfloat16), bit)
        total = keep.astype(jnp.float32) + got.astype(jnp.float32)
        return total, [b for b in have if b != bit]

    def scatter(self, whole):
        columns = whole.shape[-1]
        have = list(range(self.bits))
        values = whole.reshape((2,) * self.bits + (-1, columns))
        if self.core is not None:
            values, have = self.shrink(values, have, self.core)
            values = values.astype(jnp.bfloat16)
        cut = half_cut(columns)
        parts = []
        for piece, order in (
            (values[..., :cut], self.first[::-1]),
            (values[..., cut:], self.second[::-1]),
        ):
            held = list(have)
            for bit in order:
                piece, held = self.shrink(piece, held, bit)
                piece = piece.astype(jnp.bfloat16)
            parts.append(piece)
        values = jnp.concatenate(parts, axis=-1)
        for bit in self.shared[::-1]:
            values, held = self.shrink(values, held, bit)
        return values.astype(jnp.float32)


def build(mesh):
    fsdp = mesh.shape["fsdp"]
    experts = mesh.shape["expert"]
    cube = Cube(fsdp, experts)

    def on_device(
        tokens, expert_ids, ln1_gain, w_qkv, w_out, ln2_gain, w_router, w_in, w_back, cotangent
    ):
        images, seq_len, width = tokens.shape
        row_count = images * seq_len
        score_scale = 1.0 / math.sqrt(HD)
        slots = experts * CAP
        part_in = w_in.shape[1]
        hidden = w_in.shape[2] // fsdp

        first_block = jnp.concatenate([w_qkv, pad_lanes(ln1_gain[:, None])], axis=1)
        second_block = jnp.concatenate(
            [w_out, pad_lanes(jnp.concatenate([w_router, ln2_gain[:, None]], axis=1))], axis=1
        )
        full_first = cube.gather(first_block)
        full_second = cube.gather(second_block)
        full_qkv = full_first[:, : 3 * width]
        gain_one = full_first[:, 3 * width].astype(jnp.float32)
        full_out = full_second[:, :width]
        full_router = full_second[:, width : width + experts]
        gain_two = full_second[:, width + experts].astype(jnp.float32)

        in_pieces = jnp.transpose(w_in[0].reshape(part_in, fsdp, hidden), (1, 0, 2))
        in_slice = lax.all_to_all(in_pieces, "fsdp", split_axis=0, concat_axis=0, tiled=True)
        in_slice = in_slice.reshape(fsdp * part_in, hidden)
        back_slice = w_back[0]

        chosen_ids = expert_ids.reshape(row_count, 2)
        names = jnp.arange(experts, dtype=jnp.int32)[:, None]
        hot_first = (chosen_ids[:, 0][None, :] == names).astype(jnp.bfloat16)
        hot_second = (chosen_ids[:, 1][None, :] == names).astype(jnp.bfloat16)
        order = jnp.arange(row_count, dtype=jnp.int32)
        earlier = (order[:, None] < order[None, :]).astype(jnp.bfloat16)
        before_first = dot(hot_first, earlier, 1, 0)
        before_second = dot(hot_second, earlier, 1, 0) + jnp.sum(
            hot_first.astype(jnp.float32), axis=1, keepdims=True
        )
        place = jnp.arange(CAP, dtype=jnp.float32)[None, :, None]
        chosen = jnp.where(
            ((hot_first[:, None, :] > 0) & (before_first[:, None, :] == place))
            | ((hot_second[:, None, :] > 0) & (before_second[:, None, :] == place)),
            1.0,
            0.0,
        )
        pick = chosen.reshape(slots, row_count).astype(jnp.bfloat16)
        d_final = cotangent.reshape(row_count, width)
        d_rows = dot(pick, d_final, 1, 0)

        def send_out(rows):
            many = jnp.broadcast_to(
                rows.reshape(1, experts, CAP, width), (fsdp, experts, CAP, width)
            ).reshape(fsdp * experts, CAP, width)
            return lax.all_to_all(many, AXES, split_axis=0, concat_axis=0, tiled=True).reshape(
                -1, width
            )

        def send_back(rows):
            many = rows.reshape(fsdp * experts, CAP, width)
            many = lax.all_to_all(many, AXES, split_axis=0, concat_axis=0, tiled=True)
            return jnp.sum(many.reshape(fsdp, slots, width).astype(jnp.float32), axis=0)

        flat_x = tokens.reshape(row_count, width).astype(jnp.float32)
        normed_one, inv_one = normalize(flat_x)
        input_one = (normed_one * gain_one).astype(jnp.bfloat16)
        projected = dot(input_one, full_qkv, 1, 0, jnp.bfloat16)
        queries = projected[:, :width].reshape(images, seq_len, HEADS, HD)
        keys_all = projected[:, width : 2 * width].reshape(images, seq_len, HEADS, HD)
        values_all = projected[:, 2 * width :].reshape(images, seq_len, HEADS, HD)
        scores = (
            jnp.einsum("ishd,ithd->ihst", queries, keys_all, preferred_element_type=jnp.float32)
            * score_scale
        )
        log_total = jnp.log(jnp.sum(jnp.exp(scores), axis=-1, keepdims=True))
        weights = jnp.exp(scores - log_total)
        weights_low = weights.astype(jnp.bfloat16)
        mixed_low = (
            jnp.einsum(
                "ihst,ithd->ishd", weights_low, values_all, preferred_element_type=jnp.float32
            )
            .reshape(row_count, width)
            .astype(jnp.bfloat16)
        )
        middle = flat_x + dot(mixed_low, full_out, 1, 0)
        normed_two, inv_two = normalize(middle)
        input_two = (normed_two * gain_two).astype(jnp.bfloat16)
        exp_logits = jnp.exp(dot(full_router, input_two, 0, 1))
        probs = exp_logits / jnp.sum(exp_logits, axis=0, keepdims=True)
        slot_gate = jnp.sum(chosen * probs[:, None, :], axis=-1).reshape(slots, 1)

        arrived = send_out(dot(pick, input_two, 1, 0, jnp.bfloat16))
        d_arrived = send_out((d_rows * slot_gate).astype(jnp.bfloat16))
        hidden_pre = dot(arrived, in_slice, 1, 0)
        cdf = normal_cdf(hidden_pre)
        activated = (hidden_pre * cdf).astype(jnp.bfloat16)
        returned = send_back(dot(activated, back_slice, 1, 0, jnp.bfloat16))
        slope = cdf + hidden_pre * jnp.exp(-0.5 * hidden_pre * hidden_pre) * INV_ROOT_TAU
        d_hidden = (dot(d_arrived, back_slice, 1, 1) * slope).astype(jnp.bfloat16)
        d_returned = send_back(dot(d_hidden, in_slice, 1, 1, jnp.bfloat16))
        grad_in_part = dot(arrived, d_hidden, 0, 0, jnp.bfloat16).reshape(fsdp, part_in, hidden)
        grad_in_part = lax.all_to_all(
            grad_in_part, "fsdp", split_axis=0, concat_axis=0, tiled=True
        )
        grad_in = jnp.transpose(grad_in_part, (1, 0, 2)).reshape(1, part_in, fsdp * hidden)
        grad_in = grad_in.astype(jnp.float32)
        grad_back = dot(activated, d_arrived, 0, 0)[None]

        combined = dot(pick, (returned * slot_gate).astype(jnp.bfloat16), 0, 0)
        block_out = (middle + combined).astype(jnp.bfloat16).reshape(images, seq_len, width)
        d_gates = jnp.sum(d_rows * returned, axis=-1).reshape(experts, CAP, 1)
        d_probs = jnp.sum(chosen * d_gates, axis=1)
        d_logits = (probs * (d_probs - jnp.sum(probs * d_probs, axis=0, keepdims=True))).astype(
            jnp.bfloat16
        )
        d_input_two = dot(pick, d_returned.astype(jnp.bfloat16), 0, 0) + dot(
            d_logits, full_router, 0, 1
        )
        grad_router_full = dot(input_two, d_logits, 0, 1, jnp.bfloat16)
        d_norm_two, grad_two_full = norm_back(d_input_two, normed_two, inv_two, gain_two)
        d_middle = d_final.astype(jnp.float32) + d_norm_two
        d_middle_low = d_middle.astype(jnp.bfloat16)
        grad_out_full = dot(mixed_low, d_middle_low, 0, 0, jnp.bfloat16)
        second_full = jnp.concatenate(
            [
                grad_out_full,
                pad_lanes(
                    jnp.concatenate(
                        [grad_router_full, grad_two_full.astype(jnp.bfloat16)[:, None]], axis=1
                    )
                ),
            ],
            axis=1,
        )
        second_sum = cube.scatter(second_full)
        d_mixed = dot(d_middle_low, full_out, 1, 1, jnp.bfloat16).reshape(
            images, seq_len, HEADS, HD
        )
        mixed_wide = mixed_low.astype(jnp.float32).reshape(images, seq_len, HEADS, HD)
        delta = jnp.transpose(
            jnp.sum(d_mixed.astype(jnp.float32) * mixed_wide, axis=-1), (0, 2, 1)
        )[..., None]
        d_values = jnp.einsum(
            "ihst,ishd->ithd", weights_low, d_mixed, preferred_element_type=jnp.float32
        )
        d_weights = jnp.einsum(
            "ishd,ithd->ihst", d_mixed, values_all, preferred_element_type=jnp.float32
        )
        d_scores = (weights * (d_weights - delta)).astype(jnp.bfloat16)
        d_queries = (
            jnp.einsum("ihst,ithd->ishd", d_scores, keys_all, preferred_element_type=jnp.float32)
            * score_scale
        )
        d_keys = (
            jnp.einsum("ihst,ishd->ithd", d_scores, queries, preferred_element_type=jnp.float32)
            * score_scale
        )
        d_projected = jnp.concatenate(
            [
                d_queries.reshape(row_count, width),
                d_keys.reshape(row_count, width),
                d_values.reshape(row_count, width),
            ],
            axis=1,
        ).astype(jnp.bfloat16)
        grad_qkv = cube.scatter(dot(input_one, d_projected, 0, 0, jnp.bfloat16))
        d_input_one = dot(d_projected, full_qkv, 1, 1)
        d_norm_one, grad_one_full = norm_back(d_input_one, normed_one, inv_one, gain_one)
        grad_tokens = (d_middle + d_norm_one).reshape(images, seq_len, width)
        share = width // cube.count
        grad_one_parts = lax.all_to_all(
            grad_one_full.reshape(cube.count, 1, share), AXES, split_axis=0, concat_axis=0, tiled=True
        )
        grad_ln1 = jnp.sum(grad_one_parts, axis=(0, 1))
        return (
            block_out,
            grad_tokens,
            grad_ln1,
            grad_qkv,
            second_sum[:, :width],
            second_sum[:, width + experts],
            second_sum[:, width : width + experts],
            grad_in,
            grad_back,
        )

    return on_device


def solution(mesh):
    shared = P(AXES)
    return jax.shard_map(
        build(mesh),
        mesh=mesh,
        in_specs=(
            P(AXES, None, None),
            P(AXES, None, None),
            shared,
            P(AXES, None),
            P(AXES, None),
            shared,
            P(AXES, None),
            P("expert", "fsdp", None),
            P("expert", "fsdp", None),
            P(AXES, None, None),
        ),
        out_specs=(
            P(AXES, None, None),
            P(AXES, None, None),
            shared,
            P(AXES, None),
            P(AXES, None),
            shared,
            P(AXES, None),
            P("expert", "fsdp", None),
            P("expert", "fsdp", None),
        ),
        check_vma=False,
    )
```
